256 devices in a mesh: rows: 32 (over x, y, core), grp: 8 (over z).
Axes of the slice: x: 4, y: 4, z: 8, core: 2. Of those that a mesh axis runs over, the one named last changes fastest.
Arguments:
- residual_in: float32 [65536, 128], P(('rows', 'grp')), may hold values from -6 to 6
- solution_in: float32 [65536, 128], P(('rows', 'grp')), may hold values from -6 to 6
- descriptors: float32 [32, 65536], P(None, ('rows', 'grp')), may hold values from -6 to 6
- length_weights: float32 [32], replicated, may hold values from 0.015625 to 0.125
- amplitude: float32 [1], replicated, may hold values from 0.05 to 0.15
- noise: float32 [1], replicated, may hold values from 0.5 to 1.5
- block_inverse: float32 [2, 1024, 1024], P(None, 'grp'), may hold values from -2 to 2, as said below
- block_rows: int32 [2, 1024], replicated, may hold values from 0 to 65535, as said below
Outputs:
- solution_field: float32 [65536, 128], P(('rows', 'grp'))
- residual_field: float32 [65536, 128], P(('rows', 'grp'))
The draws below stay inside these ranges and needn't reach their ends.
Inputs may be any that keep to these rules, and one draw needn't show every extreme that they name: `block_rows`: for each step the 1024 rows are distinct; at most 16 of them lie in one device's rows (the rows of one index of rows+grp, 256 consecutive rows), and in every step some device holds exactly 16. `block_inverse`: each step's matrix is symmetric.
All inputs are finite; a program needn't handle non-finite values.
Results may differ from the reference program's by a relative error of at most 0.0001.
Values sent between devices are 32-bit elements; how exact they have to be, the bound alone decides.
A program may use at most 64 MiB of HBM per device.

```python
import math
import jax
import jax.numpy as jnp
from jax import lax

DESC = 32
RHS = 128
ROWS_DEV = 256
BLOCK = 1024
STEPS = 2
MOST = 16
NTRAIN = 65536
DEVICES = 256


def draw_block_rows(key, part):

    def draw_step(step_key):
        key_full, key_perm, key_order, key_local = jax.random.split(step_key, 4)
        full_device = jax.random.randint(key_full, (), 0, DEVICES)
        slot_total = DEVICES * MOST
        shuffled = jax.random.permutation(key_perm, slot_total)
        slot_owner = shuffled // MOST
        counter = jnp.arange(slot_total, dtype=jnp.int32)
        priority = jnp.where(slot_owner == full_device, counter - slot_total, counter)
        chosen = shuffled[jnp.argsort(priority, stable=True)[:BLOCK]]
        chosen = jax.random.permutation(key_order, chosen)
        tables = jax.vmap(lambda subkey: jax.random.permutation(subkey, ROWS_DEV)[:MOST])(jax.random.split(key_local, DEVICES))
        owners = chosen // MOST
        return (owners * ROWS_DEV + tables[owners, chosen % MOST]).astype(jnp.int32)
    return jnp.stack([draw_step(jax.random.fold_in(key, 7 + step_index)) for step_index in range(STEPS)])


def draw_block_inverse(key, part):

    def draw_step(step_key):
        key_diag, key_off = jax.random.split(step_key)
        diagonal = jax.random.uniform(key_diag, (BLOCK,), jnp.float32, 0.5, 1.5)
        gauss = jax.random.normal(key_off, (BLOCK, BLOCK), jnp.float32) * (0.5 / BLOCK ** 0.5)
        symmetric = (gauss + gauss.T) * 0.5 ** 0.5
        symmetric = jnp.clip(symmetric, -0.5, 0.5)
        return symmetric + jnp.diag(diagonal)
    return jnp.stack([draw_step(jax.random.fold_in(key, 31 + step_index)) for step_index in range(STEPS)]).astype(jnp.float32)


def level_of(key, shape, cuts, smallest, top_value):
    loudness, own = 1.0, jax.random.fold_in(key, 6)
    for dim, shards_of in cuts:
        steps = jnp.exp(jax.random.uniform(jax.random.fold_in(own, dim), (shards_of,), jnp.float32, smallest / len(cuts), top_value / len(cuts)))
        loudness = loudness * jnp.repeat(steps, shape[dim] // shards_of).reshape([-1 if axis == dim else 1 for axis in range(len(shape))])
    return loudness


def gaussian(stream_key, extent, width, limit, pieces=(), kind=jnp.bfloat16):
    entries = jax.random.normal(stream_key, extent, jnp.float32) * width
    if len(pieces) > 0:
        entries = level_of(stream_key, extent, pieces, -0.22, 0.18) * entries
    return jnp.clip(entries, min=-limit, max=limit).astype(kind)


def setup_inputs(seed: int = 0) -> dict:
    seeds = jax.random.split(jax.random.key(seed), 9)
    residual_in = gaussian(seeds[0], (NTRAIN, RHS), 1.0, 6.0, ((0, 256),), jnp.float32)
    solution_in = gaussian(seeds[1], (NTRAIN, RHS), 1.0, 6.0, ((0, 256),), jnp.float32)
    descriptors = gaussian(seeds[2], (DESC, NTRAIN), 1.0, 6.0, ((1, 256),), jnp.float32)
    length_weights = jnp.clip(jnp.exp(jax.random.uniform(seeds[3], (DESC,), jnp.float32, math.log(0.015625), math.log(0.125))), 0.015625, 0.125)
    amplitude = jnp.clip(jax.random.uniform(seeds[4], (1,), jnp.float32, 0.05, 0.15), 0.05, 0.15)
    noise = jnp.clip(jax.random.uniform(seeds[5], (1,), jnp.float32, 0.5, 1.5), 0.5, 1.5)
    block_inverse = draw_block_inverse(jax.random.fold_in(seeds[8], 71), 0)
    block_rows = draw_block_rows(jax.random.fold_in(seeds[8], 71), 0)
    return dict(residual_in=residual_in, solution_in=solution_in, descriptors=descriptors, length_weights=length_weights, amplitude=amplitude, noise=noise, block_inverse=block_inverse, block_rows=block_rows)


def kernel_tile(points, others, weights, scale_value):
    weighted = points * weights[:, None]
    cross_terms = lax.dot_general(weighted, others, (((0,), (0,)), ((), ())), precision=lax.Precision.HIGHEST)
    own_sq = jnp.sum(weighted * points, axis=0)
    other_sq = jnp.sum(others * others * weights[:, None], axis=0)
    return scale_value * jnp.exp(-(own_sq[:, None] + other_sq[None, :] - 2.0 * cross_terms))


def reference(residual_in, solution_in, descriptors, length_weights, amplitude, noise, block_inverse, block_rows):
    residual = residual_in
    solution = solution_in
    shard_count = NTRAIN // ROWS_DEV
    for step_index in range(STEPS):
        rows_now = block_rows[step_index]
        block_res = residual[rows_now]
        block_points = descriptors[:, rows_now]
        update = jnp.dot(block_inverse[step_index], block_res, precision=lax.Precision.HIGHEST)
        stacked_res = residual.reshape(shard_count, ROWS_DEV, RHS)
        stacked_pts = descriptors.reshape(DESC, shard_count, ROWS_DEV).transpose(1, 0, 2)

        def shard_update(operands):
            res_part, pts_part = operands
            kernel_block = kernel_tile(pts_part, block_points, length_weights, amplitude[0])
            return res_part - jnp.dot(kernel_block, update, precision=lax.Precision.HIGHEST)

        residual = lax.map(shard_update, (stacked_res, stacked_pts)).reshape(NTRAIN, RHS)
        residual = residual.at[rows_now].add(-noise[0] * update)
        solution = solution.at[rows_now].add(update)
    return solution, residual
```

```python
import jax
import jax.numpy as jnp
from jax import lax
from jax.experimental import pallas as pl
from jax.experimental.pallas import tpu as pltpu
from jax.sharding import PartitionSpec as P

MESH = pl.DeviceIdType.MESH
F32 = jnp.float32
BF16 = jnp.bfloat16
EXACT = lax.Precision.HIGHEST
LINES, DEPTH, CHIPS, HALF = 32, 8, 16, 4
NT = (((1,), (1,)), ((), ()))
TN = (((0,), (0,)), ((), ()))


def iota(shape, dim):
    return lax.broadcasted_iota(jnp.int32, shape, dim)


def dot(a, b, dims=(((1,), (0,)), ((), ()))):
    return lax.dot_general(a, b, dims, preferred_element_type=F32)


def parts2(x):
    high = x.astype(BF16).astype(F32)
    return high, x - high


def parts3(x):
    high = x.astype(BF16).astype(F32)
    rest = x - high
    middle = rest.astype(BF16).astype(F32)
    return high, middle, rest - middle


def stack2(x):
    return jnp.concatenate(parts2(x), axis=0).astype(BF16)


def stack3(x):
    return jnp.concatenate(parts3(x), axis=0).astype(BF16)


def left_side(points, weights):
    n = points.shape[1]
    w = weights[:, :1]
    a1, a2, a3 = parts3(2.0 * (w * points))
    s1, s2, s3 = parts3(-jnp.sum(w * points * points, axis=0, keepdims=True))
    row = iota((16, n), 0)
    tail = jnp.where(row == 0, s1, jnp.where(row == 1, s2, jnp.where(row == 2, s3, jnp.where(row < 6, 1.0, 0.0))))
    return jnp.concatenate([a1, a1, a2, a1, a2, a3, tail], axis=0).astype(BF16)


def right_side(points, weights):
    n = points.shape[1]
    w = weights[:, :1]
    b1, b2, b3 = parts3(points)
    s1, s2, s3 = parts3(-jnp.sum(w * points * points, axis=0, keepdims=True))
    row = iota((16, n), 0)
    tail = jnp.where(row < 3, 1.0, jnp.where(row == 3, s1, jnp.where(row == 4, s2, jnp.where(row == 5, s3, 0.0))))
    return jnp.concatenate([b1, b2, b1, b3, b2, b1, tail], axis=0).astype(BF16)


def small_product(x, split_matrix):
    n = split_matrix.shape[0] // 2
    out = dot(stack2(x), split_matrix, NT)
    return out[:8, :n] + out[8:, :n] + out[:8, n:]


def kernel(
    res_ref, sol_ref, desc_ref, inv_ref, rows_ref, w_ref, amp_ref, noise_ref,
    sol_out, res_out,
    cols, ids, onehot, lines, tiles, slots, points_in, part_out, part_in, right, left,
    invs, ag, solved, spread, kern,
    s_line, r_line, s_tile, r_tile, s_pts, r_pts, s_part, r_part,
    s_solved, r_solved, s_spread, r_spread, s_fwd, r_fwd,
):
    r = lax.axis_index("rows")
    z = lax.axis_index("grp")
    chip, core = lax.div(r, 2), lax.rem(r, 2)
    sibling = r + 1 - 2 * core
    base = (r * DEPTH + z) * 256
    amp = amp_ref[0]
    noise = noise_ref[0]

    barrier = pltpu.get_barrier_semaphore()

    def greet_depth(k, carry):
        pl.semaphore_signal(barrier, inc=1, device_id=(r, lax.rem(z + k, DEPTH)), device_id_type=MESH)
        return carry

    def greet_plane(k, carry):
        pl.semaphore_signal(barrier, inc=1, device_id=(lax.rem(r + k, LINES), z), device_id_type=MESH)
        return carry

    lax.fori_loop(1, DEPTH, greet_depth, 0)
    lax.fori_loop(1, LINES, greet_plane, 0)

    weights = jnp.zeros((32, 128), F32)
    for d in range(32):
        weights = jnp.where(iota((32, 128), 0) == d, w_ref[d], weights)
    picks = []
    lane = iota((1, 256), 1)
    before = (iota((256, 256), 0) < iota((256, 256), 1)).astype(F32).astype(BF16)
    for s in range(2):
        for k in range(8):
            row = rows_ref[s:s + 1, 128 * k:128 * k + 128].astype(F32)
            cols[s, 128 * k:128 * k + 128, :] = jnp.broadcast_to(row, (128, 128)).T
        member = []
        for h in range(2):
            here = (base + 128 * h + iota((1, 128), 1)).astype(F32)
            hit = jnp.where(cols[s] == here, 1.0, 0.0)
            member.append(jnp.max(hit, axis=0, keepdims=True))
        member = jnp.concatenate(member, axis=1)
        rank = dot(jnp.broadcast_to(member, (16, 256)).astype(BF16), before)
        slot = iota((16, 256), 0).astype(F32)
        picks.append(jnp.where((rank == slot) & (member > 0.5), 1.0, 0.0))
    picks = jnp.concatenate(picks, axis=0)
    picked_res = jnp.dot(picks, res_ref[...], precision=EXACT)
    desc = desc_ref[...]
    picked_pts = lax.dot_general(
        picks, jnp.concatenate([desc] * 4, axis=0), NT, precision=EXACT
    )
    quarter = lax.div(iota((8, 128), 1), 32)
    packed = jnp.zeros((8, 128), F32)
    for q in range(4):
        packed = jnp.where(quarter == q, picked_pts[8 * q:8 * q + 8], packed)
    lines[z] = jnp.concatenate([picked_res, packed], axis=0)

    pl.semaphore_wait(barrier, DEPTH - 1 + LINES - 1)

    def line_copy(k):
        return pltpu.make_async_remote_copy(
            src_ref=lines.at[z], dst_ref=lines.at[z], send_sem=s_line.at[k], recv_sem=r_line.at[k],
            device_id=(r, lax.rem(z + k, DEPTH)), device_id_type=MESH)

    for k in range(1, DEPTH):
        line_copy(k).start()

    for s in range(2):
        invs[s] = stack2(inv_ref[s])

    def slot_ids(s):
        rows = rows_ref[s:s + 1, :]
        owner = lax.shift_right_logical(rows, 8)
        first = (owner * 256).astype(F32)
        value = rows.astype(F32)

        def count(q, total):
            col = cols[s, pl.ds(pl.multiple_of(q * 128, 128), 128), :]
            out = []
            for k in range(8):
                cut = slice(128 * k, 128 * k + 128)
                hit = (col >= first[:, cut]) & (col < value[:, cut])
                out.append(jnp.sum(jnp.where(hit, 1.0, 0.0).reshape(16, 8, 128), axis=0))
            return total + jnp.concatenate(out, axis=1)

        total = lax.fori_loop(0, 8, count, jnp.zeros((8, 1024), F32))
        rank = jnp.sum(total, axis=0, keepdims=True).astype(jnp.int32)
        line = lax.shift_right_logical(owner, 3)
        ids[s:s + 1, :] = (
            (line & 1) * 2048 + lax.shift_right_logical(line, 1) * 128
            + lax.shift_right_logical(rank, 3) * 64 + (owner & 7) * 8 + (rank & 7))

    def fill_onehot(s):
        def fill(k, carry):
            for c in range(2):
                want = ids[s:s + 1, :] - (c * 2048 + k * 128)
                onehot[s, c, pl.ds(pl.multiple_of(k * 128, 128), 128), :] = jnp.where(
                    iota((128, 1024), 0) == want, 1.0, 0.0).astype(BF16)
            return carry
        lax.fori_loop(0, CHIPS, fill, 0)

    slot_ids(0)
    fill_onehot(0)

    for k in range(1, DEPTH):
        line_copy(k).wait_recv()

    turned = []
    for s in range(2):
        turned.append(jnp.concatenate(
            [lines[:, 16 * s + 8 * h:16 * s + 8 * h + 8, :].reshape(64, 128) for h in range(2)], axis=0).T)
    t0, t1 = (t.reshape(16, 8, 128) for t in turned)
    upper = iota((16, 8, 128), 1) < 4
    tiles[:, 0] = jnp.where(upper, t0, pltpu.roll(t1, 4, 1))
    tiles[:, 1] = jnp.where(upper, pltpu.roll(t0, 4, 1), t1)

    def tile_copy(k):
        to = lax.rem(r + k, LINES)
        return pltpu.make_async_remote_copy(
            src_ref=tiles.at[lax.div(to, 2), lax.rem(to, 2)], dst_ref=slots.at[core, chip],
            send_sem=s_tile.at[k], recv_sem=r_tile.at[k], device_id=(to, z), device_id_type=MESH)

    def start_tile(k, carry):
        tile_copy(k).start()
        return carry

    lax.fori_loop(1, LINES, start_tile, 0)
    slots[core, chip] = tiles[chip, core]

    a = lines[:, 32:40, :].reshape(64, 128)
    turned = jnp.concatenate([a, pltpu.roll(a, 96, 1)], axis=0).T
    points_in[chip] = jnp.concatenate([turned[:32], turned[64:96]], axis=0)

    def points_copy(k):
        return pltpu.make_async_remote_copy(
            src_ref=points_in.at[chip], dst_ref=points_in.at[chip], send_sem=s_pts.at[k], recv_sem=r_pts.at[k],
            device_id=(lax.rem(r + 2 * k, LINES), z), device_id_type=MESH)

    def start_points(k, carry):
        points_copy(k).start()
        return carry

    lax.fori_loop(1, CHIPS, start_points, 0)

    slot_ids(1)
    fill_onehot(1)
    left_own = left_side(desc, weights)

    def wait_tile(k, carry):
        tile_copy(k).wait_recv()
        return carry

    lax.fori_loop(1, LINES, wait_tile, 0)

    halves = [
        stack3(jnp.concatenate([slots[c, k] for k in range(CHIPS)], axis=1)) for c in range(2)
    ]

    def ordered(s):
        out = dot(halves[0], onehot[s, 0]) + dot(halves[1], onehot[s, 1])
        return out[:8] + out[8:16] + out[16:]

    def solved_copy(s, k):
        return pltpu.make_async_remote_copy(
            src_ref=solved.at[s, z], dst_ref=solved.at[s, z], send_sem=s_solved.at[s, k], recv_sem=r_solved.at[s, k],
            device_id=(r, lax.rem(z + k, DEPTH)), device_id_type=MESH)

    solved[0, z] = small_product(ordered(0), invs[0])
    for k in range(1, DEPTH):
        solved_copy(0, k).start()

    panel1 = small_product(pltpu.roll(ordered(1), 4, 0), invs[1])

    def wait_points(k, carry):
        points_copy(k).wait_recv()
        return carry

    lax.fori_loop(1, CHIPS, wait_points, 0)
    for s in range(2):
        block = jnp.concatenate([points_in[k, 32 * s:32 * s + 32] for k in range(CHIPS)], axis=1)
        out = dot(stack3(block), onehot[s, core])
        part_out[32 * s:32 * s + 32] = out[:32] + out[32:64] + out[64:]
    part = pltpu.make_async_remote_copy(
        src_ref=part_out, dst_ref=part_in, send_sem=s_part, recv_sem=r_part,
        device_id=(sibling, z), device_id_type=MESH)
    part.start()
    part.wait_recv()
    block_points = part_out[...] + part_in[...]
    for s in range(2):
        right[s] = right_side(block_points[32 * s:32 * s + 32], weights)
    left[...] = left_side(block_points[32:64], weights)

    total = jnp.zeros((128, 1024), F32)
    for k in range(4):
        cut = slice(256 * k, 256 * k + 256)
        tile = amp * jnp.exp(dot(left[:, cut], right[0], TN))
        rows0 = rows_ref[0:1, :].astype(F32)
        same = jnp.concatenate(
            [cols[1, cut, :] == rows0[:, 128 * m:128 * m + 128] for m in range(8)], axis=1)
        tile = tile + jnp.where(same, noise, 0.0)
        high, low = parts2(tile)
        out = dot(invs[1, :, cut], high.astype(BF16))
        total = total + out[:128] + out[128:] + dot(invs[1, :128, cut], low.astype(BF16))
    ag[...] = stack2(total)

    for k in range(1, DEPTH):
        solved_copy(0, k).wait_recv()

    def whole(s):
        return jnp.concatenate([solved[s, k] for k in range(DEPTH)], axis=1)

    def spread_copy(s, k):
        return pltpu.make_async_remote_copy(
            src_ref=spread.at[s, core, chip], dst_ref=spread.at[s, core, chip],
            send_sem=s_spread.at[s, k], recv_sem=r_spread.at[s, k],
            device_id=(lax.rem(r + 2 * k, LINES), z), device_id_type=MESH)

    def forward_copy(s, k):
        origin = lax.rem(chip + CHIPS - k, CHIPS)
        return pltpu.make_async_remote_copy(
            src_ref=spread.at[s, core, origin], dst_ref=spread.at[s, core, origin],
            send_sem=s_fwd.at[s, k], recv_sem=r_fwd.at[s, k],
            device_id=(sibling, z), device_id_type=MESH)

    def spread_out(s, mine):
        spread[s, core, chip] = jnp.where(
            iota((8, 512), 0) < 4, mine[:, :512], pltpu.roll(mine[:, 512:], 4, 0))

        def start(k, carry):
            spread_copy(s, k).start()
            return carry

        lax.fori_loop(1, CHIPS, start, 0)
        forward_copy(s, 0).start()

    def pass_on(s):
        def step(k, carry):
            spread_copy(s, k).wait_recv()
            forward_copy(s, k).start()
            return carry

        lax.fori_loop(1, CHIPS, step, 0)

    first = whole(0)
    solved[1, z] = panel1 - small_product(first, ag[...])
    for k in range(1, DEPTH):
        solved_copy(1, k).start()
    spread_out(0, first)

    for s in range(2):
        high, low = parts2(amp * jnp.exp(dot(left_own, right[s], TN)))
        kern[s, :256] = high.astype(BF16)
        kern[s, 256:512] = low.astype(BF16)
        own = iota((256, 1024), 0) + base == rows_ref[s:s + 1, :]
        kern[s, 512:] = jnp.where(own, 1.0, 0.0).astype(BF16)

    for k in range(1, DEPTH):
        solved_copy(1, k).wait_recv()
    spread_out(1, whole(1))

    def change(s):
        def wait(k, carry):
            forward_copy(s, k).wait_recv()
            return carry

        lax.fori_loop(0, CHIPS, wait, 0)
        even, odd = spread[s, 0], spread[s, 1]
        top = iota((CHIPS, 8, 512), 1) < 4
        update = jnp.concatenate([
            jnp.where(top, even, pltpu.roll(odd, 4, 1)).reshape(128, 512),
            jnp.where(top, pltpu.roll(even, 4, 1), odd).reshape(128, 512)], axis=1)
        out = dot(kern[s], stack2(update), NT)
        smooth = out[:256, :128] + out[:256, 128:] + out[256:512, :128]
        return smooth, out[512:, :128] + out[512:, 128:]

    pass_on(0)
    smooth0, own0 = change(0)
    pass_on(1)
    smooth1, own1 = change(1)
    moved = own0 + own1
    sol_out[...] = sol_ref[...] + moved
    res_out[...] = res_ref[...] - smooth0 - smooth1 - noise * moved

    for k in range(1, DEPTH):
        line_copy(k).wait_send()
        for s in range(2):
            solved_copy(s, k).wait_send()

    def drain_tiles(k, carry):
        tile_copy(k).wait_send()
        return carry

    def drain_chips(k, carry):
        points_copy(k).wait_send()
        for s in range(2):
            spread_copy(s, k).wait_send()
            forward_copy(s, k).wait_send()
        return carry

    lax.fori_loop(1, LINES, drain_tiles, 0)
    lax.fori_loop(1, CHIPS, drain_chips, 0)
    for s in range(2):
        forward_copy(s, 0).wait_send()
    part.wait_send()


def local(residual_in, solution_in, descriptors, length_weights, amplitude, noise, block_inverse, block_rows):
    vmem = pl.BlockSpec(memory_space=pltpu.VMEM)
    smem = pl.BlockSpec(memory_space=pltpu.SMEM)
    dma = pltpu.SemaphoreType.DMA
    shape = jax.ShapeDtypeStruct(residual_in.shape, F32)
    return pl.pallas_call(
        kernel,
        out_shape=(shape, shape),
        in_specs=[vmem] * 5 + [smem] * 3,
        out_specs=(vmem, vmem),
        scratch_shapes=[
            pltpu.VMEM((2, 1024, 128), F32),
            pltpu.VMEM((2, 1024), jnp.int32),
            pltpu.VMEM((2, 2, 2048, 1024), BF16),
            pltpu.VMEM((DEPTH, 40, 128), F32),
            pltpu.VMEM((CHIPS, 2, 8, 128), F32),
            pltpu.VMEM((2, CHIPS, 8, 128), F32),
            pltpu.VMEM((CHIPS, 64, 128), F32),
            pltpu.VMEM((64, 1024), F32),
            pltpu.VMEM((64, 1024), F32),
            pltpu.VMEM((2, 208, 1024), BF16),
            pltpu.VMEM((208, 1024), BF16),
            pltpu.VMEM((2, 256, 1024), BF16),
            pltpu.VMEM((256, 1024), BF16),
            pltpu.VMEM((2, DEPTH, 8, 128), F32),
            pltpu.VMEM((2, 2, CHIPS, 8, 512), F32),
            pltpu.VMEM((2, 768, 1024), BF16),
            dma((DEPTH,)), dma((DEPTH,)), dma((LINES,)), dma((LINES,)), dma((CHIPS,)), dma((CHIPS,)),
            dma, dma,
            dma((2, DEPTH)), dma((2, DEPTH)), dma((2, CHIPS)), dma((2, CHIPS)), dma((2, CHIPS)), dma((2, CHIPS)),
        ],
        compiler_params=pltpu.CompilerParams(
            collective_id=0, has_side_effects=True, vmem_limit_bytes=56 * 1024 * 1024),
    )(residual_in, solution_in, descriptors, block_inverse, block_rows, length_weights, amplitude, noise)


def solution(mesh):
    placed = (
        P(("rows", "grp"), None),
        P(("rows", "grp"), None),
        P(None, ("rows", "grp")),
        P(),
        P(),
        P(),
        P(None, "grp", None),
        P(),
    )
    return jax.shard_map(
        local,
        mesh=mesh,
        in_specs=placed,
        out_specs=(P(("rows", "grp"), None), P(("rows", "grp"), None)),
        check_vma=False,
    )
```

```python
import jax
import jax.numpy as jnp
from jax import lax
from jax.experimental import pallas as pl
from jax.experimental.pallas import tpu as pltpu
from jax.sharding import PartitionSpec as P

MESH = pl.DeviceIdType.MESH
F32 = jnp.float32
BF16 = jnp.bfloat16
LINES, DEPTH, CHIPS = 32, 8, 16
FAR_FIRST = (4, 3, 5, 2, 6, 1, 7)
OFFSETS = sorted(
    ((a, b) for a in range(4) for b in range(4) if a or b),
    key=lambda o: -(min(o[0], 4 - o[0]) + min(o[1], 4 - o[1])))
GROUPS = (OFFSETS[:5], OFFSETS[5:10], OFFSETS[10:])
VMEM_BYTES = 56 * 1024 * 1024
NT = (((1,), (1,)), ((), ()))
TN = (((0,), (0,)), ((), ()))


def iota(shape, dim):
    return lax.broadcasted_iota(jnp.int32, shape, dim)


def dot(a, b, dims=(((1,), (0,)), ((), ()))):
    return lax.dot_general(a, b, dims, preferred_element_type=F32)


def parts2(x):
    high = x.astype(BF16).astype(F32)
    return high, x - high


def parts3(x):
    high = x.astype(BF16).astype(F32)
    rest = x - high
    middle = rest.astype(BF16).astype(F32)
    return high, middle, rest - middle


def stack2(x):
    return jnp.concatenate(parts2(x), axis=0).astype(BF16)


def stack3(x):
    return jnp.concatenate(parts3(x), axis=0).astype(BF16)


def left_side(points, weights, log_amp):
    n = points.shape[1]
    w = weights[:, :1]
    a1, a2, a3 = parts3(2.0 * (w * points))
    s1, s2, s3 = parts3(log_amp - jnp.sum(w * points * points, axis=0, keepdims=True))
    row = iota((16, n), 0)
    tail = jnp.where(row == 0, s1, jnp.where(row == 1, s2, jnp.where(row == 2, s3, jnp.where(row < 6, 1.0, 0.0))))
    return jnp.concatenate([a1, a1, a2, a1, a2, a3, tail], axis=0).astype(BF16)


def right_side(points, weights):
    n = points.shape[1]
    w = weights[:, :1]
    b1, b2, b3 = parts3(points)
    s1, s2, s3 = parts3(-jnp.sum(w * points * points, axis=0, keepdims=True))
    row = iota((16, n), 0)
    tail = jnp.where(row < 3, 1.0, jnp.where(row == 3, s1, jnp.where(row == 4, s2, jnp.where(row == 5, s3, 0.0))))
    return jnp.concatenate([b1, b2, b1, b3, b2, b1, tail], axis=0).astype(BF16)


def small_product(x, split_matrix):
    n = split_matrix.shape[0] // 2
    out = dot(stack2(x), split_matrix, NT)
    return out[:8, :n] + out[8:, :n] + out[:8, n:]


def kernel(
    res_hbm, sol_hbm, desc_hbm, inv_hbm, rows_hbm, w_hbm, amp_hbm, noise_hbm,
    sol_out, res_out,
    res_ref, sol_ref, desc_ref, inv_ref, rows_ref, w_ref, amp_ref, noise_ref,
    cols, ids, onehot, lines, packs, tiles, slots, points_in, part_out, part_in, right, left,
    invs, inv_slots, noisy, ag, solved, spread, kern, load_sem, late_sem,
    s_line, r_line, s_pack, r_pack, s_tile, r_tile, s_pts, r_pts, s_part, r_part,
    s_solved, r_solved, s_spread, r_spread, s_fwd, r_fwd,
):
    r = lax.axis_index("rows")
    z = lax.axis_index("grp")
    chip, core = lax.div(r, 2), lax.rem(r, 2)
    sibling = r + 1 - 2 * core
    base = (r * DEPTH + z) * 256

    loads = [
        pltpu.make_async_copy(a, b, load_sem.at[k])
        for k, (a, b) in enumerate([
            (rows_hbm, rows_ref), (res_hbm, res_ref), (desc_hbm, desc_ref), (w_hbm, w_ref),
            (amp_hbm, amp_ref), (noise_hbm, noise_ref)])]
    late = [
        pltpu.make_async_copy(a, b, late_sem.at[k])
        for k, (a, b) in enumerate([(inv_hbm, inv_ref), (sol_hbm, sol_ref)])]
    for copy in loads + late:
        copy.start()
    barrier = pltpu.get_barrier_semaphore()

    def greet_depth(k, carry):
        for line in (r, sibling):
            pl.semaphore_signal(barrier, inc=1, device_id=(line, lax.rem(z + k, DEPTH)), device_id_type=MESH)
        return carry

    def greet_plane(k, carry):
        pl.semaphore_signal(barrier, inc=1, device_id=(lax.rem(r + k, LINES), z), device_id_type=MESH)
        return carry

    lax.fori_loop(1, DEPTH, greet_depth, 0)
    lax.fori_loop(1, LINES, greet_plane, 0)
    for copy in loads[:2]:
        copy.wait()
    before = (iota((256, 256), 0) < iota((256, 256), 1)).astype(F32).astype(BF16)

    def pick(s):
        for k in range(8):
            row = rows_ref[s:s + 1, 128 * k:128 * k + 128].astype(F32)
            cols[s, 128 * k:128 * k + 128, :] = jnp.broadcast_to(row, (128, 128)).T
        member = []
        for h in range(2):
            here = (base + 128 * h + iota((1, 128), 1)).astype(F32)
            hit = jnp.where(cols[s] == here, 1.0, 0.0)
            member.append(jnp.max(hit, axis=0, keepdims=True))
        member = jnp.concatenate(member, axis=1)
        rank = dot(jnp.broadcast_to(member, (16, 256)).astype(BF16), before)
        slot = iota((16, 256), 0).astype(F32)
        mine = jnp.where((rank == slot) & (member > 0.5), 1.0, 0.0).astype(BF16)
        out = dot(mine, split_res)
        lines[s, z] = out[:, :128] + out[:, 128:256] + out[:, 256:]
        return mine

    split_res = jnp.concatenate(parts3(res_ref[...]), axis=1).astype(BF16)
    picks = [pick(0)]
    pl.semaphore_wait(barrier, 2 * (DEPTH - 1) + LINES - 1)

    def remote(src, dst, send, recv, to):
        return pltpu.make_async_remote_copy(
            src_ref=src, dst_ref=dst, send_sem=send, recv_sem=recv, device_id=to, device_id_type=MESH)

    def along(k):
        return (r, lax.rem(z + k, DEPTH))

    def line_copy(s, k):
        return remote(lines.at[s, z], lines.at[s, z], s_line.at[s], r_line.at[s], along(k))

    def all_lines(s):
        return remote(lines.at[s, 0:DEPTH - 1], lines.at[s, 0:DEPTH - 1], s_line.at[s], r_line.at[s], along(1))

    def pack_copy(k):
        return remote(packs.at[z], packs.at[z], s_pack, r_pack, along(k))

    all_packs = remote(packs.at[0:DEPTH - 1], packs.at[0:DEPTH - 1], s_pack, r_pack, along(1))

    for k in FAR_FIRST:
        line_copy(0, k).start()
    picks.append(pick(1))
    for copy in loads[2:]:
        copy.wait()
    noise = noise_ref[0]
    weights = jnp.zeros((32, 128), F32)
    for d in range(32):
        weights = jnp.where(iota((32, 128), 0) == d, w_ref[d], weights)
    log_amp = jnp.log(jnp.broadcast_to(amp_ref[0], (1, 128)))[:, :1]
    desc = desc_ref[...]
    wide = jnp.concatenate([part for part in parts3(desc) for _ in range(4)], axis=0).astype(BF16)
    out = jnp.concatenate([dot(mine, wide, NT) for mine in picks], axis=0)
    picked_pts = out[:, :128] + out[:, 128:256] + out[:, 256:]
    quarter = lax.div(iota((8, 128), 1), 32)
    packed = jnp.zeros((8, 128), F32)
    for q in range(4):
        packed = jnp.where(quarter == q, picked_pts[8 * q:8 * q + 8], packed)
    packs[z] = packed
    for k in FAR_FIRST:
        pack_copy(k).start()
    for k in FAR_FIRST:
        line_copy(1, k).start()

    late[0].wait()
    for s in range(2):
        invs[s] = stack2(inv_ref[s])

    def slot_ids(s):
        rows = rows_ref[s:s + 1, :]
        owner = lax.shift_right_logical(rows, 8)
        first = (owner * 256).astype(F32)
        value = rows.astype(F32)

        def count(q, total):
            col = cols[s, pl.ds(pl.multiple_of(q * 128, 128), 128), :]
            out = []
            for k in range(8):
                cut = slice(128 * k, 128 * k + 128)
                hit = (col >= first[:, cut]) & (col < value[:, cut])
                out.append(jnp.sum(jnp.where(hit, 1.0, 0.0).reshape(16, 8, 128), axis=0))
            return total + jnp.concatenate(out, axis=1)

        total = lax.fori_loop(0, 8, count, jnp.zeros((8, 1024), F32))
        rank = jnp.sum(total, axis=0, keepdims=True).astype(jnp.int32)
        line = lax.shift_right_logical(owner, 3)
        ids[s:s + 1, :] = (
            (line & 1) * 2048 + lax.shift_right_logical(line, 1) * 128
            + lax.shift_right_logical(rank, 3) * 64 + (owner & 7) * 8 + (rank & 7))

    def fill_onehot(s):
        def fill(k, carry):
            want = ids[s:s + 1, :] - (core * 2048 + k * 128)
            onehot[s, pl.ds(pl.multiple_of(k * 128, 128), 128), :] = jnp.where(
                iota((128, 1024), 0) == want, 1.0, 0.0).astype(BF16)
            return carry
        lax.fori_loop(0, CHIPS, fill, 0)

    slot_ids(0)
    fill_onehot(0)

    def make_tiles(s):
        tiles[s] = jnp.concatenate(
            [lines[s, :, 8 * h:8 * h + 8, :].reshape(64, 128) for h in range(2)], axis=0).T.reshape(CHIPS, 8, 128)

    def shifted(offset, sign=1):
        a, b = offset
        x, y = lax.div(chip, 4), lax.rem(chip, 4)
        return lax.rem(x + 4 + sign * a, 4) * 4 + lax.rem(y + 4 + sign * b, 4)

    def tile_copy(s, to):
        return remote(tiles.at[s, to], slots.at[s, chip], s_tile.at[s], r_tile.at[s], (2 * to + core, z))

    def all_tiles(s):
        return remote(slots.at[s, 0:CHIPS - 1], slots.at[s, 0:CHIPS - 1], s_tile.at[s], r_tile.at[s], (sibling, z))

    def send_tiles(s):
        for offset in OFFSETS:
            tile_copy(s, shifted(offset)).start()
        slots[s, chip] = tiles[s, chip]

    def across(offset):
        return (2 * shifted(offset) + core, z)

    side = lax.div(chip, 8)

    def points_copy(k):
        return remote(points_in.at[chip], points_in.at[chip], s_pts, r_pts.at[side], across(k))

    def some_points(n, h):
        return remote(points_in.at[0:n], points_in.at[0:n], s_pts, r_pts.at[h], (sibling, z))

    all_lines(0).wait_recv()
    make_tiles(0)
    send_tiles(0)
    all_packs.wait_recv()
    a = packs[...].reshape(64, 128)
    turned = jnp.concatenate([a, pltpu.roll(a, 96, 1)], axis=0).T
    points_in[chip] = jnp.concatenate([turned[:32], turned[64:96]], axis=0)
    for offset in OFFSETS:
        points_copy(offset).start()
    all_lines(1).wait_recv()
    make_tiles(1)
    send_tiles(1)

    inv_slots[...] = dot(invs[0], onehot[0], NT).astype(BF16)
    slot_ids(1)
    fill_onehot(1)
    first_row = pl.multiple_of(512 * core, 512)
    mine = cols[1, pl.ds(first_row, 512), :]
    rows0 = rows_ref[0:1, :].astype(F32)
    same = jnp.concatenate(
        [jnp.where(mine == rows0[:, 128 * m:128 * m + 128], 1.0, 0.0).astype(BF16) for m in range(8)], axis=1)
    out = dot(invs[1, :, pl.ds(first_row, 512)], same)
    noisy[...] = noise * (out[:128] + out[128:])
    left_own = left_side(desc, weights, log_amp)

    def side_by_side(s):
        return jnp.concatenate([slots[s, k] for k in range(CHIPS)], axis=1)

    def solved_copy(s, to):
        here = solved.at[s, core * DEPTH + z]
        return remote(here, here, s_solved.at[s], r_solved.at[s], to)

    def send_solved(s):
        for k in FAR_FIRST:
            for line in (r, sibling):
                solved_copy(s, (line, lax.rem(z + k, DEPTH))).start()
        solved_copy(s, (sibling, z)).start()

    def all_solved(s):
        here = solved.at[s, 0:2 * DEPTH - 1]
        return remote(here, here, s_solved.at[s], r_solved.at[s], (sibling, z))

    all_tiles(0).wait_recv()
    solved[0, core * DEPTH + z] = small_product(side_by_side(0), inv_slots[...])
    send_solved(0)

    for n in range(2):
        h = 1 - side if n == 0 else side
        some_points(8 - n, h).wait_recv()
        for s in range(2):
            block = jnp.concatenate([points_in[8 * h + k, 32 * s:32 * s + 32] for k in range(8)], axis=1)
            out = dot(stack3(block), onehot[s, pl.ds(pl.multiple_of(1024 * h, 1024), 1024), :])
            out = out[:32] + out[32:64] + out[64:]
            part_out[32 * s:32 * s + 32] = out if n == 0 else part_out[32 * s:32 * s + 32] + out
    part = remote(part_out, part_in, s_part, r_part, (sibling, z))
    part.start()
    all_tiles(1).wait_recv()
    out = dot(stack3(side_by_side(1)), onehot[1])
    panel1 = small_product(out[:8] + out[8:16] + out[16:], invs[1])
    part.wait_recv()
    block_points = part_out[...] + part_in[...]
    for s in range(2):
        right[s] = right_side(block_points[32 * s:32 * s + 32], weights)
    left[...] = left_side(block_points[32:64], weights, log_amp)

    total = noisy[...]
    for k in range(2):
        cut = pl.ds(pl.multiple_of(512 * core + 256 * k, 256), 256)
        high, low = parts2(jnp.exp(dot(left[:, cut], right[0], TN)))
        out = dot(invs[1, :, cut], high.astype(BF16))
        total = total + out[:128] + out[128:] + dot(invs[1, :128, cut], low.astype(BF16))
    ag[...] = stack2(total)

    def whole(s):
        return jnp.concatenate([solved[s, k] + solved[s, DEPTH + k] for k in range(DEPTH)], axis=1)

    def spread_copy(s, k, g):
        here = spread.at[s, core, chip]
        return remote(here, here, s_spread.at[s], r_spread.at[s, g], across(k))

    def group_spread(s, g):
        here = spread.at[s, 0, 0:len(GROUPS[g])]
        return remote(here, here, s_spread.at[s], r_spread.at[s, g], (sibling, z))

    def all_sent(s):
        here = spread.at[s, 0, 0:CHIPS - 1]
        return remote(here, here, s_spread.at[s], r_spread.at[s, 0], (sibling, z))

    def forward_copy(s, k):
        here = spread.at[s, core, shifted(k, -1)]
        return remote(here, here, s_fwd.at[s], r_fwd.at[s], (sibling, z))

    def all_forward(s):
        return remote(spread.at[s, 0], spread.at[s, 0], s_fwd.at[s], r_fwd.at[s], (sibling, z))

    def spread_out(s):
        spread[s, core, chip] = solved[s, pl.ds(4 * core, 4)] + solved[s, pl.ds(DEPTH + 4 * core, 4)]
        for g, group in enumerate(GROUPS):
            for k in group:
                spread_copy(s, k, g).start()
        forward_copy(s, (0, 0)).start()

    def pass_on(s):
        for g, group in enumerate(GROUPS):
            group_spread(s, g).wait_recv()
            for k in group:
                forward_copy(s, k).start()

    all_solved(0).wait_recv()
    solved[1, core * DEPTH + z] = panel1 - small_product(whole(0), ag[...])
    send_solved(1)
    spread_out(0)

    for s in range(2):
        high, low = parts2(jnp.exp(dot(left_own, right[s], TN)))
        kern[s, :256] = high.astype(BF16)
        kern[s, 256:512] = low.astype(BF16)
        own = iota((256, 1024), 0) + base == rows_ref[s:s + 1, :]
        kern[s, 512:] = jnp.where(own, 1.0, 0.0).astype(BF16)

    all_solved(1).wait_recv()
    spread_out(1)

    def change(s, h):
        update = jnp.concatenate([spread[s, h, :, k].reshape(128, 128) for k in range(4)], axis=1)
        out = dot(kern[s, :, pl.ds(pl.multiple_of(512 * h, 512), 512)], stack2(update), NT)
        smooth = out[:256, :128] + out[:256, 128:] + out[256:512, :128]
        return smooth, out[512:, :128] + out[512:, 128:]

    late[1].wait()
    smooth, moved = jnp.zeros((256, 128), F32), jnp.zeros((256, 128), F32)
    for s in range(2):
        pass_on(s)
        for h in (core, 1 - core):
            if h is not core:
                all_forward(s).wait_recv()
            more = change(s, h)
            smooth, moved = smooth + more[0], moved + more[1]
    sol_out[...] = sol_ref[...] + moved
    res_out[...] = res_ref[...] - smooth - noise * moved

    all_packs.wait_send()
    some_points(CHIPS - 1, 0).wait_send()
    part.wait_send()
    for s in range(2):
        all_lines(s).wait_send()
        all_tiles(s).wait_send()
        all_solved(s).wait_send()
        all_sent(s).wait_send()
        all_forward(s).wait_send()


def local(residual_in, solution_in, descriptors, length_weights, amplitude, noise, block_inverse, block_rows):
    vmem = pl.BlockSpec(memory_space=pltpu.VMEM)
    hbm = pl.BlockSpec(memory_space=pl.ANY)
    dma = pltpu.SemaphoreType.DMA
    shape = pltpu.VMEM(residual_in.shape, F32)
    return pl.pallas_call(
        kernel,
        out_shape=(shape, shape),
        in_specs=[hbm] * 8,
        out_specs=(vmem, vmem),
        scratch_shapes=[
            pltpu.VMEM((256, 128), F32),
            pltpu.VMEM((256, 128), F32),
            pltpu.VMEM((32, 256), F32),
            pltpu.VMEM((2, 128, 1024), F32),
            pltpu.VMEM((2, 1024), jnp.int32),
            pltpu.SMEM((32,), F32),
            pltpu.SMEM((1,), F32),
            pltpu.SMEM((1,), F32),
            pltpu.VMEM((2, 1024, 128), F32),
            pltpu.VMEM((2, 1024), jnp.int32),
            pltpu.VMEM((2, 2048, 1024), BF16),
            pltpu.VMEM((2, DEPTH, 16, 128), F32),
            pltpu.VMEM((DEPTH, 8, 128), F32),
            pltpu.VMEM((2, CHIPS, 8, 128), F32),
            pltpu.VMEM((2, CHIPS, 8, 128), F32),
            pltpu.VMEM((CHIPS, 64, 128), F32),
            pltpu.VMEM((64, 1024), F32),
            pltpu.VMEM((64, 1024), F32),
            pltpu.VMEM((2, 208, 1024), BF16),
            pltpu.VMEM((208, 1024), BF16),
            pltpu.VMEM((2, 256, 1024), BF16),
            pltpu.VMEM((256, 2048), BF16),
            pltpu.VMEM((128, 1024), F32),
            pltpu.VMEM((256, 1024), BF16),
            pltpu.VMEM((2, 2 * DEPTH, 8, 128), F32),
            pltpu.VMEM((2, 2, CHIPS, 4, 8, 128), F32),
            pltpu.VMEM((2, 768, 1024), BF16),
            dma((6,)), dma((2,)),
            dma((2,)), dma((2,)), dma, dma, dma((2,)), dma((2,)), dma, dma((2,)), dma, dma,
            dma((2,)), dma((2,)), dma((2,)), dma((2, len(GROUPS))), dma((2,)), dma((2,)),
        ],
        compiler_params=pltpu.CompilerParams(
            collective_id=0, has_side_effects=True, vmem_limit_bytes=VMEM_BYTES),
    )(residual_in, solution_in, descriptors, block_inverse, block_rows, length_weights, amplitude, noise)


def solution(mesh):
    placed = (
        P(("rows", "grp"), None),
        P(("rows", "grp"), None),
        P(None, ("rows", "grp")),
        P(),
        P(),
        P(),
        P(None, "grp", None),
        P(),
    )
    return jax.shard_map(
        local,
        mesh=mesh,
        in_specs=placed,
        out_specs=(P(("rows", "grp"), None), P(("rows", "grp"), None)),
        check_vma=False,
    )
```

```python
import jax
import jax.numpy as jnp
from jax import lax
from jax.experimental import pallas as pl
from jax.experimental.pallas import tpu as pltpu
from jax.sharding import PartitionSpec as P

MESH = pl.DeviceIdType.MESH
F32 = jnp.float32
BF16 = jnp.bfloat16
LINES, DEPTH, CHIPS = 32, 8, 16
FAR_FIRST = (4, 3, 5, 2, 6, 1, 7)
ORDER = (0, 1, 7, 2, 3, 5, 4, 6)
OFFSETS = sorted(
    ((a, b) for a in range(4) for b in range(4) if a or b),
    key=lambda o: -(min(o[0], 4 - o[0]) + min(o[1], 4 - o[1])))
VMEM_BYTES = 56 * 1024 * 1024
NT = (((1,), (1,)), ((), ()))
TN = (((0,), (0,)), ((), ()))


def iota(shape, dim):
    return lax.broadcasted_iota(jnp.int32, shape, dim)


def dot(a, b, dims=(((1,), (0,)), ((), ()))):
    return lax.dot_general(a, b, dims, preferred_element_type=F32)


def parts2(x):
    high = x.astype(BF16).astype(F32)
    return high, x - high


def parts3(x):
    high = x.astype(BF16).astype(F32)
    rest = x - high
    middle = rest.astype(BF16).astype(F32)
    return high, middle, rest - middle


def stack2(x):
    return jnp.concatenate(parts2(x), axis=0).astype(BF16)


def stack3(x):
    return jnp.concatenate(parts3(x), axis=0).astype(BF16)


def left_side(points, weights, log_amp):
    n = points.shape[1]
    w = weights[:, :1]
    a1, a2, a3 = parts3(2.0 * (w * points))
    s1, s2, s3 = parts3(log_amp - jnp.sum(w * points * points, axis=0, keepdims=True))
    row = iota((16, n), 0)
    tail = jnp.where(row == 0, s1, jnp.where(row == 1, s2, jnp.where(row == 2, s3, jnp.where(row < 6, 1.0, 0.0))))
    return jnp.concatenate([a1, a1, a2, a1, a2, a3, tail], axis=0).astype(BF16)


def right_side(points, weights):
    n = points.shape[1]
    w = weights[:, :1]
    b1, b2, b3 = parts3(points)
    s1, s2, s3 = parts3(-jnp.sum(w * points * points, axis=0, keepdims=True))
    row = iota((16, n), 0)
    tail = jnp.where(row < 3, 1.0, jnp.where(row == 3, s1, jnp.where(row == 4, s2, jnp.where(row == 5, s3, 0.0))))
    return jnp.concatenate([b1, b2, b1, b3, b2, b1, tail], axis=0).astype(BF16)


def small_product(x, split_matrix):
    n = split_matrix.shape[0] // 2
    out = dot(stack2(x), split_matrix, NT)
    return out[:8, :n] + out[8:, :n] + out[:8, n:]


def kernel(
    res_hbm, sol_hbm, desc_hbm, inv_hbm, rows_hbm, w_hbm, amp_hbm, noise_hbm,
    sol_out, res_out,
    res_ref, sol_ref, desc_ref, inv_ref, rows_ref, w_ref, amp_ref, noise_ref,
    cols, ids, onehot, lines, packs, tiles, slots, points_in, part_out, part_in, right, left,
    invs, inv_slots, noisy, ag, solved, spread, kern, load_sem, late_sem,
    s_line, r_line, s_pack, r_pack, s_tile, r_tile, s_pts, r_pts, s_part, r_part,
    s_solved, r_solved, s_spread, r_spread, s_fwd, r_fwd,
):
    r = lax.axis_index("rows")
    z = lax.axis_index("grp")
    chip, core = lax.div(r, 2), lax.rem(r, 2)
    sibling = r + 1 - 2 * core
    base = (r * DEPTH + z) * 256
    panels = [pl.multiple_of(128 * lax.rem(z + q, DEPTH), 128) for q in ORDER]

    loads = [
        pltpu.make_async_copy(a, b, load_sem.at[k])
        for k, (a, b) in enumerate([
            (rows_hbm, rows_ref), (res_hbm, res_ref), (desc_hbm, desc_ref), (w_hbm, w_ref),
            (amp_hbm, amp_ref), (noise_hbm, noise_ref)])]
    late = [
        pltpu.make_async_copy(a, b, late_sem.at[k])
        for k, (a, b) in enumerate([(inv_hbm, inv_ref), (sol_hbm, sol_ref)])]
    for copy in loads + late:
        copy.start()
    barrier = pltpu.get_barrier_semaphore()

    def greet_depth(k, carry):
        for line in (r, sibling):
            pl.semaphore_signal(barrier, inc=1, device_id=(line, lax.rem(z + k, DEPTH)), device_id_type=MESH)
        return carry

    def greet_plane(k, carry):
        pl.semaphore_signal(barrier, inc=1, device_id=(lax.rem(r + k, LINES), z), device_id_type=MESH)
        return carry

    lax.fori_loop(1, DEPTH, greet_depth, 0)
    lax.fori_loop(1, LINES, greet_plane, 0)
    loads[0].wait()
    before = (iota((256, 256), 0) < iota((256, 256), 1)).astype(F32).astype(BF16)

    def pick(s):
        for k in range(8):
            row = rows_ref[s:s + 1, 128 * k:128 * k + 128].astype(F32)
            cols[s, 128 * k:128 * k + 128, :] = jnp.broadcast_to(row, (128, 128)).T
        member = []
        for h in range(2):
            here = (base + 128 * h + iota((1, 128), 1)).astype(F32)
            hit = jnp.where(cols[s] == here, 1.0, 0.0)
            member.append(jnp.max(hit, axis=0, keepdims=True))
        member = jnp.concatenate(member, axis=1)
        rank = dot(jnp.broadcast_to(member, (16, 256)).astype(BF16), before)
        slot = iota((16, 256), 0).astype(F32)
        return jnp.where((rank == slot) & (member > 0.5), 1.0, 0.0).astype(BF16)

    def fill_line(s):
        out = dot(picks[s], split_res)
        lines[s, z] = out[:, :128] + out[:, 128:256] + out[:, 256:]

    picks = [pick(0)]
    loads[1].wait()
    split_res = jnp.concatenate(parts3(res_ref[...]), axis=1).astype(BF16)
    fill_line(0)
    pl.semaphore_wait(barrier, 2 * (DEPTH - 1) + LINES - 1)

    def remote(src, dst, send, recv, to):
        return pltpu.make_async_remote_copy(
            src_ref=src, dst_ref=dst, send_sem=send, recv_sem=recv, device_id=to, device_id_type=MESH)

    def along(k):
        return (r, lax.rem(z + k, DEPTH))

    def line_copy(s, k):
        return remote(lines.at[s, z], lines.at[s, z], s_line.at[s], r_line.at[s], along(k))

    def all_lines(s):
        return remote(lines.at[s, 0:DEPTH - 1], lines.at[s, 0:DEPTH - 1], s_line.at[s], r_line.at[s], along(1))

    def pack_copy(k):
        return remote(packs.at[z], packs.at[z], s_pack, r_pack, along(k))

    all_packs = remote(packs.at[0:DEPTH - 1], packs.at[0:DEPTH - 1], s_pack, r_pack, along(1))

    for k in FAR_FIRST:
        line_copy(0, k).start()
    picks.append(pick(1))
    fill_line(1)
    for copy in loads[2:]:
        copy.wait()
    noise = noise_ref[0]
    weights = jnp.zeros((32, 128), F32)
    for d in range(32):
        weights = jnp.where(iota((32, 128), 0) == d, w_ref[d], weights)
    log_amp = jnp.log(jnp.broadcast_to(amp_ref[0], (1, 128)))[:, :1]
    desc = desc_ref[...]
    wide = jnp.concatenate([part for part in parts3(desc) for _ in range(4)], axis=0).astype(BF16)
    out = jnp.concatenate([dot(mine, wide, NT) for mine in picks], axis=0)
    picked_pts = out[:, :128] + out[:, 128:256] + out[:, 256:]
    quarter = lax.div(iota((8, 128), 1), 32)
    packed = jnp.zeros((8, 128), F32)
    for q in range(4):
        packed = jnp.where(quarter == q, picked_pts[8 * q:8 * q + 8], packed)
    packs[z] = packed
    for k in FAR_FIRST:
        pack_copy(k).start()
    for k in FAR_FIRST:
        line_copy(1, k).start()

    late[0].wait()
    for s in range(2):
        invs[s] = stack2(inv_ref[s])

    def rows_in_order(s):
        return jnp.concatenate([rows_ref[s:s + 1, pl.ds(p, 128)] for p in panels], axis=1)

    def slot_ids(s):
        rows = rows_ref[s:s + 1, :]
        owner = lax.shift_right_logical(rows, 8)
        first = (owner * 256).astype(F32)
        value = rows.astype(F32)

        def count(q, total):
            col = cols[s, pl.ds(pl.multiple_of(q * 128, 128), 128), :]
            out = []
            for k in range(8):
                cut = slice(128 * k, 128 * k + 128)
                hit = (col >= first[:, cut]) & (col < value[:, cut])
                out.append(jnp.sum(jnp.where(hit, 1.0, 0.0).reshape(16, 8, 128), axis=0))
            return total + jnp.concatenate(out, axis=1)

        total = lax.fori_loop(0, 8, count, jnp.zeros((8, 1024), F32))
        rank = jnp.sum(total, axis=0, keepdims=True).astype(jnp.int32)
        line = lax.shift_right_logical(owner, 3)
        ids[s:s + 1, :] = (
            (line & 1) * 2048 + lax.shift_right_logical(line, 1) * 128
            + lax.shift_right_logical(rank, 3) * 64 + (owner & 7) * 8 + (rank & 7))

    def fill_onehot(s):
        def fill(k, carry):
            want = ids[s:s + 1, :] - (core * 2048 + k * 128)
            onehot[s, pl.ds(pl.multiple_of(k * 128, 128), 128), :] = jnp.where(
                iota((128, 1024), 0) == want, 1.0, 0.0).astype(BF16)
            return carry
        lax.fori_loop(0, CHIPS, fill, 0)

    slot_ids(0)
    fill_onehot(0)

    def make_tiles(s):
        tiles[s] = jnp.concatenate(
            [lines[s, :, 8 * h:8 * h + 8, :].reshape(64, 128) for h in range(2)], axis=0).T.reshape(CHIPS, 8, 128)

    def shifted(offset, sign=1):
        a, b = offset
        x, y = lax.div(chip, 4), lax.rem(chip, 4)
        return lax.rem(x + 4 + sign * a, 4) * 4 + lax.rem(y + 4 + sign * b, 4)

    def tile_copy(s, to):
        return remote(tiles.at[s, to], slots.at[s, chip], s_tile.at[s], r_tile.at[s], (2 * to + core, z))

    def all_tiles(s):
        return remote(slots.at[s, 0:CHIPS - 1], slots.at[s, 0:CHIPS - 1], s_tile.at[s], r_tile.at[s], (sibling, z))

    def send_tiles(s):
        for offset in OFFSETS:
            tile_copy(s, shifted(offset)).start()
        slots[s, chip] = tiles[s, chip]

    def across(offset):
        return (2 * shifted(offset) + core, z)

    side = lax.div(chip, 8)

    def points_copy(k):
        return remote(points_in.at[chip], points_in.at[chip], s_pts, r_pts.at[side], across(k))

    def some_points(n, h):
        return remote(points_in.at[0:n], points_in.at[0:n], s_pts, r_pts.at[h], (sibling, z))

    all_lines(0).wait_recv()
    make_tiles(0)
    send_tiles(0)
    all_packs.wait_recv()
    a = packs[...].reshape(64, 128)
    turned = jnp.concatenate([a, pltpu.roll(a, 96, 1)], axis=0).T
    points_in[chip] = jnp.concatenate([turned[:32], turned[64:96]], axis=0)
    for offset in OFFSETS:
        points_copy(offset).start()
    all_lines(1).wait_recv()
    make_tiles(1)
    send_tiles(1)

    inv_slots[...] = dot(invs[0], onehot[0], NT).astype(BF16)
    slot_ids(1)
    fill_onehot(1)
    first_row = pl.multiple_of(512 * core, 512)
    mine = cols[1, pl.ds(first_row, 512), :]
    rows0 = rows_in_order(0).astype(F32)
    same = jnp.concatenate(
        [jnp.where(mine == rows0[:, 128 * m:128 * m + 128], 1.0, 0.0).astype(BF16) for m in range(8)], axis=1)
    out = dot(invs[1, :, pl.ds(first_row, 512)], same)
    noisy[...] = noise * (out[:128] + out[128:])
    left_own = left_side(desc, weights, log_amp)

    def side_by_side(s):
        return jnp.concatenate([slots[s, k] for k in range(CHIPS)], axis=1)

    def solved_copy(s, k, line):
        slot = ORDER.index((DEPTH - k) % DEPTH)
        return remote(
            solved.at[s, core * DEPTH], solved.at[s, core * DEPTH + slot],
            s_solved.at[s], r_solved.at[s, slot // 4], (line, lax.rem(z + k, DEPTH)))

    def send_solved(s):
        for k in FAR_FIRST:
            for line in (r, sibling):
                solved_copy(s, k, line).start()
        solved_copy(s, 0, sibling).start()

    def some_solved(s, n, far):
        here = solved.at[s, 0:n]
        return remote(here, here, s_solved.at[s], r_solved.at[s, far], (sibling, z))

    def near_solved(s):
        some_solved(s, 7, 0).wait_recv()

    def far_solved(s):
        some_solved(s, 8, 1).wait_recv()

    all_tiles(0).wait_recv()
    solved[0, core * DEPTH] = small_product(side_by_side(0), inv_slots[...])
    send_solved(0)

    def part_copy(s):
        return remote(part_out.at[s], part_in.at[s], s_part.at[s], r_part.at[s], (sibling, z))

    for n in range(2):
        h = 1 - side if n == 0 else side
        some_points(8 - n, h).wait_recv()
        for s in range(2):
            block = jnp.concatenate([points_in[8 * h + k, 32 * s:32 * s + 32] for k in range(8)], axis=1)
            out = dot(stack3(block), onehot[s, pl.ds(pl.multiple_of(1024 * h, 1024), 1024), :])
            out = out[:32] + out[32:64] + out[64:]
            part_out[s] = out if n == 0 else part_out[s] + out
            if n == 1:
                part_copy(s).start()
    all_tiles(1).wait_recv()
    out = dot(stack3(side_by_side(1)), onehot[1])
    panel1 = small_product(out[:8] + out[8:16] + out[16:], invs[1])
    for s in range(2):
        part_copy(s).wait_recv()
        right[s] = right_side(
            jnp.concatenate([part_out[s, :, pl.ds(p, 128)] + part_in[s, :, pl.ds(p, 128)] for p in panels], axis=1),
            weights)
    left[...] = left_side(part_out[1] + part_in[1], weights, log_amp)

    total = noisy[...]
    for k in range(2):
        cut = pl.ds(pl.multiple_of(512 * core + 256 * k, 256), 256)
        high, low = parts2(jnp.exp(dot(left[:, cut], right[0], TN)))
        out = dot(invs[1, :, cut], high.astype(BF16))
        total = total + out[:128] + out[128:] + dot(invs[1, :128, cut], low.astype(BF16))
    ag[...] = stack2(total)

    def whole(s):
        return jnp.concatenate([solved[s, k] + solved[s, DEPTH + k] for k in range(DEPTH)], axis=1)

    row_of_chips = lax.div(chip, 4)

    def spread_copy(s, offset):
        here = spread.at[s, core, chip]
        return remote(here, here, s_spread.at[s], r_spread.at[s, row_of_chips], across(offset))

    def some_spread(s, n, source):
        here = spread.at[s, 0, 0:n]
        return remote(here, here, s_spread.at[s], r_spread.at[s, source], (sibling, z))

    def forward_copy(s, source):
        here = spread.at[s, core, pl.ds(4 * source, 4)]
        return remote(here, here, s_fwd.at[s], r_fwd.at[s], (sibling, z))

    def all_forward(s):
        return remote(spread.at[s, 0], spread.at[s, 0], s_fwd.at[s], r_fwd.at[s], (sibling, z))

    def spread_out(s):
        spread[s, core, chip] = solved[s, pl.ds(4 * core, 4)] + solved[s, pl.ds(DEPTH + 4 * core, 4)]
        for offset in OFFSETS:
            spread_copy(s, offset).start()

    def pass_on(s):
        for k in (0, 1, 3, 2):
            source = lax.rem(row_of_chips + k, 4)
            some_spread(s, 4 if k else 3, source).wait_recv()
            forward_copy(s, source).start()

    near_solved(0)
    far_solved(0)
    solved[1, core * DEPTH] = panel1 - small_product(whole(0), ag[...])
    send_solved(1)
    spread_out(0)

    for s in range(2):
        high, low = parts2(jnp.exp(dot(left_own, right[s], TN)))
        kern[s, :256] = high.astype(BF16)
        kern[s, 256:512] = low.astype(BF16)
        own = iota((256, 1024), 0) + base == rows_in_order(s)
        kern[s, 512:] = jnp.where(own, 1.0, 0.0).astype(BF16)

    @pl.when(core == 0)
    def _():
        near_solved(1)

    @pl.when(core == 1)
    def _():
        far_solved(1)

    spread_out(1)

    def change(s, h):
        update = jnp.concatenate([spread[s, h, :, k].reshape(128, 128) for k in range(4)], axis=1)
        out = dot(kern[s, :, pl.ds(pl.multiple_of(512 * h, 512), 512)], stack2(update), NT)
        smooth = out[:256, :128] + out[:256, 128:] + out[256:512, :128]
        return smooth, out[512:, :128] + out[512:, 128:]

    late[1].wait()
    smooth, moved = jnp.zeros((256, 128), F32), jnp.zeros((256, 128), F32)
    for s in range(2):
        pass_on(s)
        for h in (core, 1 - core):
            if h is not core:
                all_forward(s).wait_recv()
            more = change(s, h)
            smooth, moved = smooth + more[0], moved + more[1]
    sol_out[...] = sol_ref[...] + moved
    res_out[...] = res_ref[...] - smooth - noise * moved

    @pl.when(core == 0)
    def _():
        far_solved(1)

    @pl.when(core == 1)
    def _():
        near_solved(1)

    all_packs.wait_send()
    some_points(CHIPS - 1, 0).wait_send()
    for s in range(2):
        part_copy(s).wait_send()
    for s in range(2):
        all_lines(s).wait_send()
        all_tiles(s).wait_send()
        some_solved(s, 15, 0).wait_send()
        some_spread(s, CHIPS - 1, 0).wait_send()
        all_forward(s).wait_send()


def local(residual_in, solution_in, descriptors, length_weights, amplitude, noise, block_inverse, block_rows):
    vmem = pl.BlockSpec(memory_space=pltpu.VMEM)
    hbm = pl.BlockSpec(memory_space=pl.ANY)
    dma = pltpu.SemaphoreType.DMA
    shape = pltpu.VMEM(residual_in.shape, F32)
    return pl.pallas_call(
        kernel,
        out_shape=(shape, shape),
        in_specs=[hbm] * 8,
        out_specs=(vmem, vmem),
        scratch_shapes=[
            pltpu.VMEM((256, 128), F32),
            pltpu.VMEM((256, 128), F32),
            pltpu.VMEM((32, 256), F32),
            pltpu.VMEM((2, 128, 1024), F32),
            pltpu.VMEM((2, 1024), jnp.int32),
            pltpu.SMEM((32,), F32),
            pltpu.SMEM((1,), F32),
            pltpu.SMEM((1,), F32),
            pltpu.VMEM((2, 1024, 128), F32),
            pltpu.VMEM((2, 1024), jnp.int32),
            pltpu.VMEM((2, 2048, 1024), BF16),
            pltpu.VMEM((2, DEPTH, 16, 128), F32),
            pltpu.VMEM((DEPTH, 8, 128), F32),
            pltpu.VMEM((2, CHIPS, 8, 128), F32),
            pltpu.VMEM((2, CHIPS, 8, 128), F32),
            pltpu.VMEM((CHIPS, 64, 128), F32),
            pltpu.VMEM((2, 32, 1024), F32),
            pltpu.VMEM((2, 32, 1024), F32),
            pltpu.VMEM((2, 208, 1024), BF16),
            pltpu.VMEM((208, 1024), BF16),
            pltpu.VMEM((2, 256, 1024), BF16),
            pltpu.VMEM((256, 2048), BF16),
            pltpu.VMEM((128, 1024), F32),
            pltpu.VMEM((256, 1024), BF16),
            pltpu.VMEM((2, 2 * DEPTH, 8, 128), F32),
            pltpu.VMEM((2, 2, CHIPS, 4, 8, 128), F32),
            pltpu.VMEM((2, 768, 1024), BF16),
            dma((6,)), dma((2,)),
            dma((2,)), dma((2,)), dma, dma, dma((2,)), dma((2,)), dma, dma((2,)), dma((2,)), dma((2,)),
            dma((2,)), dma((2, 2)), dma((2,)), dma((2, 4)), dma((2,)), dma((2,)),
        ],
        compiler_params=pltpu.CompilerParams(
            collective_id=0, has_side_effects=True, vmem_limit_bytes=VMEM_BYTES),
    )(residual_in, solution_in, descriptors, block_inverse, block_rows, length_weights, amplitude, noise)


def solution(mesh):
    placed = (
        P(("rows", "grp"), None),
        P(("rows", "grp"), None),
        P(None, ("rows", "grp")),
        P(),
        P(),
        P(),
        P(None, "grp", None),
        P(),
    )
    return jax.shard_map(
        local,
        mesh=mesh,
        in_specs=placed,
        out_specs=(P(("rows", "grp"), None), P(("rows", "grp"), None)),
        check_vma=False,
    )
```

```python
import jax
import jax.numpy as jnp
from jax import lax
from jax.experimental import pallas as pl
from jax.experimental.pallas import tpu as pltpu
from jax.sharding import PartitionSpec as P

MESH = pl.DeviceIdType.MESH
F32 = jnp.float32
BF16 = jnp.bfloat16
LINES, DEPTH, CHIPS = 32, 8, 16
FAR_FIRST = (4, 3, 5, 2, 6, 1, 7)
ORDER = (0, 1, 7, 2, 3, 5, 4, 6)
OFFSETS = sorted(
    ((a, b) for a in range(4) for b in range(4) if a or b),
    key=lambda o: -(min(o[0], 4 - o[0]) + min(o[1], 4 - o[1])))
GROUPS = (OFFSETS[:5], OFFSETS[5:10], OFFSETS[10:])
VMEM_BYTES = 56 * 1024 * 1024
NT = (((1,), (1,)), ((), ()))
TN = (((0,), (0,)), ((), ()))


def iota(shape, dim):
    return lax.broadcasted_iota(jnp.int32, shape, dim)


def dot(a, b, dims=(((1,), (0,)), ((), ()))):
    return lax.dot_general(a, b, dims, preferred_element_type=F32)


def parts2(x):
    high = x.astype(BF16).astype(F32)
    return high, x - high


def parts3(x):
    high = x.astype(BF16).astype(F32)
    rest = x - high
    middle = rest.astype(BF16).astype(F32)
    return high, middle, rest - middle


def stack2(x):
    return jnp.concatenate(parts2(x), axis=0).astype(BF16)


def stack3(x):
    return jnp.concatenate(parts3(x), axis=0).astype(BF16)


def left_side(points, weights, log_amp):
    n = points.shape[1]
    w = weights[:, :1]
    a1, a2, a3 = parts3(2.0 * (w * points))
    s1, s2, s3 = parts3(log_amp - jnp.sum(w * points * points, axis=0, keepdims=True))
    row = iota((16, n), 0)
    tail = jnp.where(row == 0, s1, jnp.where(row == 1, s2, jnp.where(row == 2, s3, jnp.where(row < 6, 1.0, 0.0))))
    return jnp.concatenate([a1, a1, a2, a1, a2, a3, tail], axis=0).astype(BF16)


def right_side(points, weights):
    n = points.shape[1]
    w = weights[:, :1]
    b1, b2, b3 = parts3(points)
    s1, s2, s3 = parts3(-jnp.sum(w * points * points, axis=0, keepdims=True))
    row = iota((16, n), 0)
    tail = jnp.where(row < 3, 1.0, jnp.where(row == 3, s1, jnp.where(row == 4, s2, jnp.where(row == 5, s3, 0.0))))
    return jnp.concatenate([b1, b2, b1, b3, b2, b1, tail], axis=0).astype(BF16)


def small_product(x, split_matrix):
    n = split_matrix.shape[0] // 2
    out = dot(stack2(x), split_matrix, NT)
    return out[:8, :n] + out[8:, :n] + out[:8, n:]


def kernel(
    res_hbm, sol_hbm, desc_hbm, inv_hbm, rows_hbm, w_hbm, amp_hbm, noise_hbm,
    sol_out, res_out,
    res_ref, sol_ref, desc_ref, inv_ref, rows_ref, w_ref, amp_ref, noise_ref,
    cols, ids, onehot, lines, packs, tiles, slots, points_in, part_out, part_in, right, left,
    invs, inv_slots, noisy, ag, solved, spread, kern, load_sem, late_sem,
    s_line, r_line, s_pack, r_pack, s_tile, r_tile, s_pts, r_pts, s_part, r_part,
    s_solved, r_solved, s_spread, r_spread, s_fwd, r_fwd,
):
    r = lax.axis_index("rows")
    z = lax.axis_index("grp")
    chip, core = lax.div(r, 2), lax.rem(r, 2)
    sibling = r + 1 - 2 * core
    base = (r * DEPTH + z) * 256
    panels = [pl.multiple_of(128 * lax.rem(z + q, DEPTH), 128) for q in ORDER]

    loads = [
        pltpu.make_async_copy(a, b, load_sem.at[k])
        for k, (a, b) in enumerate([
            (rows_hbm, rows_ref), (res_hbm, res_ref), (desc_hbm, desc_ref), (w_hbm, w_ref),
            (amp_hbm, amp_ref), (noise_hbm, noise_ref)])]
    late = [
        pltpu.make_async_copy(a, b, late_sem.at[k])
        for k, (a, b) in enumerate([(inv_hbm, inv_ref), (sol_hbm, sol_ref)])]
    for copy in loads + late:
        copy.start()
    barrier = pltpu.get_barrier_semaphore()

    def greet_depth(k, carry):
        for line in (r, sibling):
            pl.semaphore_signal(barrier, inc=1, device_id=(line, lax.rem(z + k, DEPTH)), device_id_type=MESH)
        return carry

    def greet_plane(k, carry):
        pl.semaphore_signal(barrier, inc=1, device_id=(lax.rem(r + k, LINES), z), device_id_type=MESH)
        return carry

    lax.fori_loop(1, DEPTH, greet_depth, 0)
    lax.fori_loop(1, LINES, greet_plane, 0)
    for copy in loads[:2]:
        copy.wait()
    before = (iota((256, 256), 0) < iota((256, 256), 1)).astype(F32).astype(BF16)

    def pick(s):
        for k in range(8):
            row = rows_ref[s:s + 1, 128 * k:128 * k + 128].astype(F32)
            cols[s, 128 * k:128 * k + 128, :] = jnp.broadcast_to(row, (128, 128)).T
        member = []
        for h in range(2):
            here = (base + 128 * h + iota((1, 128), 1)).astype(F32)
            hit = jnp.where(cols[s] == here, 1.0, 0.0)
            member.append(jnp.max(hit, axis=0, keepdims=True))
        member = jnp.concatenate(member, axis=1)
        rank = dot(jnp.broadcast_to(member, (16, 256)).astype(BF16), before)
        slot = iota((16, 256), 0).astype(F32)
        mine = jnp.where((rank == slot) & (member > 0.5), 1.0, 0.0).astype(BF16)
        out = dot(mine, split_res)
        lines[s, z] = out[:, :128] + out[:, 128:256] + out[:, 256:]
        return mine

    split_res = jnp.concatenate(parts3(res_ref[...]), axis=1).astype(BF16)
    picks = [pick(0)]
    pl.semaphore_wait(barrier, 2 * (DEPTH - 1) + LINES - 1)

    def remote(src, dst, send, recv, to):
        return pltpu.make_async_remote_copy(
            src_ref=src, dst_ref=dst, send_sem=send, recv_sem=recv, device_id=to, device_id_type=MESH)

    def along(k):
        return (r, lax.rem(z + k, DEPTH))

    def line_copy(s, k):
        return remote(lines.at[s, z], lines.at[s, z], s_line.at[s], r_line.at[s], along(k))

    def all_lines(s):
        return remote(lines.at[s, 0:DEPTH - 1], lines.at[s, 0:DEPTH - 1], s_line.at[s], r_line.at[s], along(1))

    def pack_copy(k):
        return remote(packs.at[z], packs.at[z], s_pack, r_pack, along(k))

    all_packs = remote(packs.at[0:DEPTH - 1], packs.at[0:DEPTH - 1], s_pack, r_pack, along(1))

    for k in FAR_FIRST:
        line_copy(0, k).start()
    picks.append(pick(1))
    for copy in loads[2:]:
        copy.wait()
    noise = noise_ref[0]
    weights = jnp.zeros((32, 128), F32)
    for d in range(32):
        weights = jnp.where(iota((32, 128), 0) == d, w_ref[d], weights)
    log_amp = jnp.log(jnp.broadcast_to(amp_ref[0], (1, 128)))[:, :1]
    desc = desc_ref[...]
    wide = jnp.concatenate([part for part in parts3(desc) for _ in range(4)], axis=0).astype(BF16)
    out = jnp.concatenate([dot(mine, wide, NT) for mine in picks], axis=0)
    picked_pts = out[:, :128] + out[:, 128:256] + out[:, 256:]
    quarter = lax.div(iota((8, 128), 1), 32)
    packed = jnp.zeros((8, 128), F32)
    for q in range(4):
        packed = jnp.where(quarter == q, picked_pts[8 * q:8 * q + 8], packed)
    packs[z] = packed
    for k in FAR_FIRST:
        pack_copy(k).start()
    for k in FAR_FIRST:
        line_copy(1, k).start()

    late[0].wait()
    for s in range(2):
        invs[s] = stack2(inv_ref[s])

    def rows_in_order(s):
        return jnp.concatenate([rows_ref[s:s + 1, pl.ds(p, 128)] for p in panels], axis=1)

    def slot_ids(s):
        rows = rows_ref[s:s + 1, :]
        owner = lax.shift_right_logical(rows, 8)
        first = (owner * 256).astype(F32)
        value = rows.astype(F32)

        def count(q, total):
            col = cols[s, pl.ds(pl.multiple_of(q * 128, 128), 128), :]
            out = []
            for k in range(8):
                cut = slice(128 * k, 128 * k + 128)
                hit = (col >= first[:, cut]) & (col < value[:, cut])
                out.append(jnp.sum(jnp.where(hit, 1.0, 0.0).reshape(16, 8, 128), axis=0))
            return total + jnp.concatenate(out, axis=1)

        total = lax.fori_loop(0, 8, count, jnp.zeros((8, 1024), F32))
        rank = jnp.sum(total, axis=0, keepdims=True).astype(jnp.int32)
        line = lax.shift_right_logical(owner, 3)
        ids[s:s + 1, :] = (
            (line & 1) * 2048 + lax.shift_right_logical(line, 1) * 128
            + lax.shift_right_logical(rank, 3) * 64 + (owner & 7) * 8 + (rank & 7))

    def fill_onehot(s):
        def fill(k, carry):
            want = ids[s:s + 1, :] - (core * 2048 + k * 128)
            onehot[s, pl.ds(pl.multiple_of(k * 128, 128), 128), :] = jnp.where(
                iota((128, 1024), 0) == want, 1.0, 0.0).astype(BF16)
            return carry
        lax.fori_loop(0, CHIPS, fill, 0)

    slot_ids(0)
    fill_onehot(0)

    def make_tiles(s):
        tiles[s] = jnp.concatenate(
            [lines[s, :, 8 * h:8 * h + 8, :].reshape(64, 128) for h in range(2)], axis=0).T.reshape(CHIPS, 8, 128)

    def shifted(offset, sign=1):
        a, b = offset
        x, y = lax.div(chip, 4), lax.rem(chip, 4)
        return lax.rem(x + 4 + sign * a, 4) * 4 + lax.rem(y + 4 + sign * b, 4)

    def tile_copy(s, to):
        return remote(tiles.at[s, to], slots.at[s, chip], s_tile.at[s], r_tile.at[s], (2 * to + core, z))

    def all_tiles(s):
        return remote(slots.at[s, 0:CHIPS - 1], slots.at[s, 0:CHIPS - 1], s_tile.at[s], r_tile.at[s], (sibling, z))

    def send_tiles(s):
        for offset in OFFSETS:
            tile_copy(s, shifted(offset)).start()
        slots[s, chip] = tiles[s, chip]

    def across(offset):
        return (2 * shifted(offset) + core, z)

    side = lax.div(chip, 8)

    def points_copy(k):
        return remote(points_in.at[chip], points_in.at[chip], s_pts, r_pts.at[side], across(k))

    def some_points(n, h):
        return remote(points_in.at[0:n], points_in.at[0:n], s_pts, r_pts.at[h], (sibling, z))

    all_lines(0).wait_recv()
    make_tiles(0)
    send_tiles(0)
    all_packs.wait_recv()
    a = packs[...].reshape(64, 128)
    turned = jnp.concatenate([a, pltpu.roll(a, 96, 1)], axis=0).T
    points_in[chip] = jnp.concatenate([turned[:32], turned[64:96]], axis=0)
    for offset in OFFSETS:
        points_copy(offset).start()
    all_lines(1).wait_recv()
    make_tiles(1)
    send_tiles(1)

    inv_slots[...] = dot(invs[0], onehot[0], NT).astype(BF16)
    slot_ids(1)
    fill_onehot(1)
    first_row = pl.multiple_of(512 * core, 512)
    mine = cols[1, pl.ds(first_row, 512), :]
    rows0 = rows_in_order(0).astype(F32)
    same = jnp.concatenate(
        [jnp.where(mine == rows0[:, 128 * m:128 * m + 128], 1.0, 0.0).astype(BF16) for m in range(8)], axis=1)
    out = dot(invs[1, :, pl.ds(first_row, 512)], same)
    noisy[...] = noise * (out[:128] + out[128:])
    left_own = left_side(desc, weights, log_amp)

    def side_by_side(s):
        return jnp.concatenate([slots[s, k] for k in range(CHIPS)], axis=1)

    def solved_copy(s, k, line):
        slot = ORDER.index((DEPTH - k) % DEPTH)
        return remote(
            solved.at[s, core * DEPTH], solved.at[s, core * DEPTH + slot],
            s_solved.at[s], r_solved.at[s, slot // 4], (line, lax.rem(z + k, DEPTH)))

    def send_solved(s):
        for k in FAR_FIRST:
            for line in (r, sibling):
                solved_copy(s, k, line).start()
        solved_copy(s, 0, sibling).start()

    def some_solved(s, n, far):
        here = solved.at[s, 0:n]
        return remote(here, here, s_solved.at[s], r_solved.at[s, far], (sibling, z))

    def near_solved(s):
        some_solved(s, 7, 0).wait_recv()

    def far_solved(s):
        some_solved(s, 8, 1).wait_recv()

    all_tiles(0).wait_recv()
    solved[0, core * DEPTH] = small_product(side_by_side(0), inv_slots[...])
    send_solved(0)

    for n in range(2):
        h = 1 - side if n == 0 else side
        some_points(8 - n, h).wait_recv()
        for s in range(2):
            block = jnp.concatenate([points_in[8 * h + k, 32 * s:32 * s + 32] for k in range(8)], axis=1)
            out = dot(stack3(block), onehot[s, pl.ds(pl.multiple_of(1024 * h, 1024), 1024), :])
            out = out[:32] + out[32:64] + out[64:]
            part_out[32 * s:32 * s + 32] = out if n == 0 else part_out[32 * s:32 * s + 32] + out
    part = remote(part_out, part_in, s_part, r_part, (sibling, z))
    part.start()
    all_tiles(1).wait_recv()
    out = dot(stack3(side_by_side(1)), onehot[1])
    panel1 = small_product(out[:8] + out[8:16] + out[16:], invs[1])
    part.wait_recv()
    for s in range(2):
        right[s] = right_side(jnp.concatenate(
            [part_out[32 * s:32 * s + 32, pl.ds(p, 128)] + part_in[32 * s:32 * s + 32, pl.ds(p, 128)] for p in panels],
            axis=1), weights)
        if s == 0:
            left[...] = left_side(part_out[32:] + part_in[32:], weights, log_amp)

    total = noisy[...]
    for k in range(2):
        cut = pl.ds(pl.multiple_of(512 * core + 256 * k, 256), 256)
        high, low = parts2(jnp.exp(dot(left[:, cut], right[0], TN)))
        out = dot(invs[1, :, cut], high.astype(BF16))
        total = total + out[:128] + out[128:] + dot(invs[1, :128, cut], low.astype(BF16))
    ag[...] = stack2(total)

    def whole(s):
        return jnp.concatenate([solved[s, k] + solved[s, DEPTH + k] for k in range(DEPTH)], axis=1)

    def spread_copy(s, k, g):
        here = spread.at[s, core, chip]
        return remote(here, here, s_spread.at[s], r_spread.at[s, g], across(k))

    def group_spread(s, g):
        here = spread.at[s, 0, 0:len(GROUPS[g])]
        return remote(here, here, s_spread.at[s], r_spread.at[s, g], (sibling, z))

    def all_sent(s):
        here = spread.at[s, 0, 0:CHIPS - 1]
        return remote(here, here, s_spread.at[s], r_spread.at[s, 0], (sibling, z))

    def forward_copy(s, k):
        here = spread.at[s, core, shifted(k, -1)]
        return remote(here, here, s_fwd.at[s], r_fwd.at[s], (sibling, z))

    def all_forward(s):
        return remote(spread.at[s, 0], spread.at[s, 0], s_fwd.at[s], r_fwd.at[s], (sibling, z))

    def spread_out(s):
        spread[s, core, chip] = solved[s, pl.ds(4 * core, 4)] + solved[s, pl.ds(DEPTH + 4 * core, 4)]
        for g, group in enumerate(GROUPS):
            for k in group:
                spread_copy(s, k, g).start()
        forward_copy(s, (0, 0)).start()

    def pass_on(s):
        for g, group in enumerate(GROUPS):
            group_spread(s, g).wait_recv()
            for k in group:
                forward_copy(s, k).start()

    near_solved(0)
    far_solved(0)
    solved[1, core * DEPTH] = panel1 - small_product(whole(0), ag[...])
    send_solved(1)
    spread_out(0)

    for s in range(2):
        high, low = parts2(jnp.exp(dot(left_own, right[s], TN)))
        kern[s, :256] = high.astype(BF16)
        kern[s, 256:512] = low.astype(BF16)
        own = iota((256, 1024), 0) + base == rows_in_order(s)
        kern[s, 512:] = jnp.where(own, 1.0, 0.0).astype(BF16)

    @pl.when(core == 0)
    def _():
        near_solved(1)

    @pl.when(core == 1)
    def _():
        far_solved(1)

    spread_out(1)

    def change(s, h):
        update = jnp.concatenate([spread[s, h, :, k].reshape(128, 128) for k in range(4)], axis=1)
        out = dot(kern[s, :, pl.ds(pl.multiple_of(512 * h, 512), 512)], stack2(update), NT)
        smooth = out[:256, :128] + out[:256, 128:] + out[256:512, :128]
        return smooth, out[512:, :128] + out[512:, 128:]

    late[1].wait()
    smooth, moved = jnp.zeros((256, 128), F32), jnp.zeros((256, 128), F32)
    for s in range(2):
        pass_on(s)
        for h in (core, 1 - core):
            if h is not core:
                all_forward(s).wait_recv()
            more = change(s, h)
            smooth, moved = smooth + more[0], moved + more[1]
    sol_out[...] = sol_ref[...] + moved
    res_out[...] = res_ref[...] - smooth - noise * moved

    @pl.when(core == 0)
    def _():
        far_solved(1)

    @pl.when(core == 1)
    def _():
        near_solved(1)

    all_packs.wait_send()
    some_points(CHIPS - 1, 0).wait_send()
    part.wait_send()
    for s in range(2):
        all_lines(s).wait_send()
        all_tiles(s).wait_send()
        some_solved(s, 15, 0).wait_send()
        all_sent(s).wait_send()
        all_forward(s).wait_send()


def local(residual_in, solution_in, descriptors, length_weights, amplitude, noise, block_inverse, block_rows):
    vmem = pl.BlockSpec(memory_space=pltpu.VMEM)
    hbm = pl.BlockSpec(memory_space=pl.ANY)
    dma = pltpu.SemaphoreType.DMA
    shape = pltpu.VMEM(residual_in.shape, F32)
    return pl.pallas_call(
        kernel,
        out_shape=(shape, shape),
        in_specs=[hbm] * 8,
        out_specs=(vmem, vmem),
        scratch_shapes=[
            pltpu.VMEM((256, 128), F32),
            pltpu.VMEM((256, 128), F32),
            pltpu.VMEM((32, 256), F32),
            pltpu.VMEM((2, 128, 1024), F32),
            pltpu.VMEM((2, 1024), jnp.int32),
            pltpu.SMEM((32,), F32),
            pltpu.SMEM((1,), F32),
            pltpu.SMEM((1,), F32),
            pltpu.VMEM((2, 1024, 128), F32),
            pltpu.VMEM((2, 1024), jnp.int32),
            pltpu.VMEM((2, 2048, 1024), BF16),
            pltpu.VMEM((2, DEPTH, 16, 128), F32),
            pltpu.VMEM((DEPTH, 8, 128), F32),
            pltpu.VMEM((2, CHIPS, 8, 128), F32),
            pltpu.VMEM((2, CHIPS, 8, 128), F32),
            pltpu.VMEM((CHIPS, 64, 128), F32),
            pltpu.VMEM((64, 1024), F32),
            pltpu.VMEM((64, 1024), F32),
            pltpu.VMEM((2, 208, 1024), BF16),
            pltpu.VMEM((208, 1024), BF16),
            pltpu.VMEM((2, 256, 1024), BF16),
            pltpu.VMEM((256, 2048), BF16),
            pltpu.VMEM((128, 1024), F32),
            pltpu.VMEM((256, 1024), BF16),
            pltpu.VMEM((2, 2 * DEPTH, 8, 128), F32),
            pltpu.VMEM((2, 2, CHIPS, 4, 8, 128), F32),
            pltpu.VMEM((2, 768, 1024), BF16),
            dma((6,)), dma((2,)),
            dma((2,)), dma((2,)), dma, dma, dma((2,)), dma((2,)), dma, dma((2,)), dma, dma,
            dma((2,)), dma((2, 2)), dma((2,)), dma((2, len(GROUPS))), dma((2,)), dma((2,)),
        ],
        compiler_params=pltpu.CompilerParams(
            collective_id=0, has_side_effects=True, vmem_limit_bytes=VMEM_BYTES),
    )(residual_in, solution_in, descriptors, block_inverse, block_rows, length_weights, amplitude, noise)


def solution(mesh):
    placed = (
        P(("rows", "grp"), None),
        P(("rows", "grp"), None),
        P(None, ("rows", "grp")),
        P(),
        P(),
        P(),
        P(None, "grp", None),
        P(),
    )
    return jax.shard_map(
        local,
        mesh=mesh,
        in_specs=placed,
        out_specs=(P(("rows", "grp"), None), P(("rows", "grp"), None)),
        check_vma=False,
    )
```
